512 devices in a mesh: band: 8 (over z), facet: 64 (over x, y, core).
Axes of the slice: x: 4, y: 8, z: 8, core: 2. Of those that a mesh axis runs over, the one named last changes fastest.
Arguments:
- facets: bfloat16 [8, 64, 2, 128, 4096], P('band', 'facet'), may hold values from -6 to 6
- col_window: float32 [4096], replicated, may hold values from 0.25 to 1
- slot_of_subgrid: int32 [96], replicated, may hold values from 0 to 127, as said below
- block_slot: int32 [8, 64, 4], P('band', 'facet'), may hold values from 0 to 1
- block_band: int32 [8, 64, 4], P('band', 'facet'), may hold values from 0 to 6
- block_offset: int32 [8, 64, 4], P('band', 'facet'), may hold values from 0 to 128
- block_weight: float32 [8, 64, 4], P('band', 'facet'), may hold values from 0 to 1
- vis_pos: float32 [8, 64, 4, 2, 2048], P('band', 'facet'), may hold values from 0 to 1
Outputs:
- subgrids: bfloat16 [8, 128, 2, 16, 256], P('band', 'facet')
- visibilities: float32 [8, 64, 4, 2, 2048], P('band', 'facet')
The draws below stay inside these ranges and needn't reach their ends.
Inputs may be any that keep to these rules, and one draw needn't show every extreme that they name: `slot_of_subgrid`: values are distinct; at most 2 subgrids share an owner, and some owner holds 2.
All inputs are finite; a program needn't handle non-finite values.
Results may differ from the reference program's by a relative error of at most 0.009.
Values may be sent and summed in bfloat16 or wider, within the bound.
A program may use at most 64 MiB of HBM per device.

```python
import math
import jax
import jax.numpy as jnp
from jax import lax

SR = 128
SL = 4096
SG = 256
CR = 16
CAP = 2
VB = 4
NV = 2048
PC = 128
NS = 96
N_BAND = 8
N_FACET = 64


def draw_slot_of_subgrid(key, part):
    first_key = jax.random.fold_in(key, 11)
    second_key = jax.random.fold_in(key, 23)
    total = N_FACET * CAP
    shuffled = jax.random.permutation(first_key, total).astype(jnp.int32)
    full_owner = shuffled[0] // CAP
    ranking = jnp.where(shuffled // CAP == full_owner, 0, 1).astype(jnp.int32)
    order = jnp.argsort(ranking, stable=True)
    chosen = shuffled[order][:NS]
    placing = jax.random.permutation(second_key, NS)
    return jnp.zeros((NS,), jnp.int32).at[placing].set(chosen).astype(jnp.int32)


def place_ends(entries, own_key, smallest, top_value):
    extent = entries.shape
    place = [jax.random.randint(jax.random.fold_in(own_key, axis), (), 0, extent[axis]) for axis in range(len(extent))]
    entries = entries.at[tuple(place)].set(smallest)
    longest = extent.index(max(extent))
    place[longest] = (place[longest] + 1) % extent[longest]
    return entries.at[tuple(place)].set(top_value)


def levels(rng, dims, cuts, smallest, largest):
    level, own = 1.0, jax.random.fold_in(rng, 6)
    for axis_at, parts in cuts:
        steps = jnp.exp(jax.random.uniform(jax.random.fold_in(own, axis_at), (parts,), jnp.float32, smallest / len(cuts), largest / len(cuts)))
        level = level * jnp.repeat(steps, dims[axis_at] // parts).reshape([-1 if axis == axis_at else 1 for axis in range(len(dims))])
    return level


def noise(stream_key, extent, deviation, reach, cuts=(), kind=jnp.bfloat16):
    entries = deviation * jax.random.normal(stream_key, extent, jnp.float32)
    if cuts:
        entries = entries * levels(stream_key, extent, cuts, -0.22, 0.18)
    return jnp.clip(entries, -reach, reach).astype(kind)


def setup_inputs(seed: int = 0) -> dict:
    keys = jax.random.split(jax.random.key(seed), 9)
    facets = noise(keys[0], (N_BAND, N_FACET, 2, SR, SL), 1.0, 6.0, ((0, 8), (1, 64)))
    col_window = jnp.clip(jax.random.uniform(keys[1], (SL,), jnp.float32, 0.25, 1.0), 0.25, 1.0)
    slot_of_subgrid = draw_slot_of_subgrid(jax.random.fold_in(keys[8], 71), 0)
    block_slot = place_ends(jax.random.randint(keys[3], (N_BAND, N_FACET, VB), 0, CAP), jax.random.fold_in(keys[3], 1), 0, CAP - 1).astype(jnp.int32)
    block_band = place_ends(jax.random.randint(keys[4], (N_BAND, N_FACET, VB), 0, N_BAND - 1), jax.random.fold_in(keys[4], 1), 0, (N_BAND - 1) - 1).astype(jnp.int32)
    block_offset = place_ends(jax.random.randint(keys[5], (N_BAND, N_FACET, VB), 0, SG - PC + 1), jax.random.fold_in(keys[5], 1), 0, SG - PC).astype(jnp.int32)
    block_weight = jnp.clip(1.0 * jax.random.uniform(keys[6], (N_BAND, N_FACET, VB), jnp.float32) ** levels(keys[6], (N_BAND, N_FACET, VB), ((0, 8), (1, 64)), -0.2, 0.2), 0.0, 1.0)
    vis_pos = jnp.clip(1.0 * jax.random.uniform(keys[7], (N_BAND, N_FACET, VB, 2, NV), jnp.float32) ** levels(keys[7], (N_BAND, N_FACET, VB, 2, NV), ((0, 8), (1, 64)), -0.2, 0.2), 0.0, 1.0)
    return {"facets": facets, "col_window": col_window, "slot_of_subgrid": slot_of_subgrid, "block_slot": block_slot, "block_band": block_band, "block_offset": block_offset, "block_weight": block_weight, "vis_pos": vis_pos}


kernel_sigma = 1.5
highest = lax.Precision.HIGHEST

def column_table(length, width):
    rows = jnp.arange(length, dtype=jnp.int32)[:, None]
    cols = jnp.arange(width, dtype=jnp.int32)[None, :]
    angle = 2.0 * math.pi / length * (rows * cols % length).astype(jnp.float32)
    return jnp.concatenate([jnp.cos(angle), -jnp.sin(angle)], axis=1).astype(jnp.bfloat16)

def combine(product, height, width):
    real_part = product[..., :height, :width] - product[..., height:, width:]
    imag_part = product[..., :height, width:] + product[..., height:, :width]
    return jnp.stack([real_part, imag_part], axis=-3)

def sky_phases(freqs, cells, total):
    angle = 2.0 * math.pi / total * (freqs[..., None] * cells % total).astype(jnp.float32)
    return jnp.concatenate([jnp.cos(angle), -jnp.sin(angle)], axis=-2).astype(jnp.bfloat16)

def inverse_columns(sigma):
    width = sigma.shape[-1]
    index = jnp.arange(width, dtype=jnp.int32)
    angle = 2.0 * math.pi / width * (index[:, None] * index[None, :] % width).astype(jnp.float32)
    cos_part = jnp.cos(angle) / math.sqrt(width)
    sin_part = jnp.sin(angle) / math.sqrt(width)
    real_in = sigma[..., 0, :, :]
    imag_in = sigma[..., 1, :, :]
    real_part = jnp.matmul(real_in, cos_part, precision=highest) - jnp.matmul(imag_in, sin_part, precision=highest)
    imag_part = jnp.matmul(real_in, sin_part, precision=highest) + jnp.matmul(imag_in, cos_part, precision=highest)
    return jnp.stack([real_part, imag_part], axis=-3).astype(jnp.bfloat16)

def degrid_block(patch, position):
    row_grid = jnp.arange(patch.shape[1], dtype=jnp.float32)[:, None]
    col_grid = jnp.arange(patch.shape[2], dtype=jnp.float32)[:, None]
    row_diff = row_grid - position[0][None, :] * (patch.shape[1] - 1)
    col_diff = col_grid - position[1][None, :] * (patch.shape[2] - 1)
    row_kernel = jnp.exp(-row_diff * row_diff / (2.0 * kernel_sigma * kernel_sigma))
    col_kernel = jnp.exp(-col_diff * col_diff / (2.0 * kernel_sigma * kernel_sigma))
    partial_sum = jnp.einsum('xrc,rv->xcv', patch, row_kernel, precision=highest)
    return lax.optimization_barrier(jnp.sum(partial_sum * col_kernel[None], axis=1))

def reference(facets, col_window, slot_of_subgrid, block_slot, block_band, block_offset, block_weight, vis_pos):
    band_count = facets.shape[0]
    facet_count = facets.shape[1]
    strip_rows = facets.shape[3]
    strip_length = facets.shape[4]
    subgrid_count = slot_of_subgrid.shape[0]
    sky_rows = facet_count * strip_rows
    table = column_table(strip_length, SG).astype(jnp.float32)
    all_cells = jnp.arange(sky_rows, dtype=jnp.int32)

    def facet_spectrum(one_facet):
        windowed = (one_facet.astype(jnp.float32) * col_window).astype(jnp.bfloat16)
        flat = windowed.reshape(2 * strip_rows, strip_length).astype(jnp.float32)
        product = jnp.dot(flat, table, precision=highest)
        return (combine(product, strip_rows, SG) * (1.0 / math.sqrt(strip_length))).astype(jnp.bfloat16)

    def band_subgrids(band_facets):
        spectra = lax.map(facet_spectrum, band_facets)
        spectrum_cat = jnp.concatenate([spectra[:, 0], spectra[:, 1]], axis=-1).astype(jnp.float32)

        def one_subgrid(index):
            freqs = index * CR + jnp.arange(CR, dtype=jnp.int32)
            phases = sky_phases(freqs, all_cells, sky_rows).astype(jnp.float32)
            phases = phases.reshape(2 * CR, facet_count, strip_rows)
            product = jnp.einsum('kfj,fjd->fkd', phases, spectrum_cat, precision=highest)
            terms = (combine(product, CR, SG) * (1.0 / math.sqrt(sky_rows))).astype(jnp.bfloat16)
            sigma = lax.optimization_barrier(jnp.sum(terms.astype(jnp.float32), axis=0))
            return inverse_columns(sigma)
        made = lax.map(one_subgrid, jnp.arange(subgrid_count, dtype=jnp.int32))
        empty = jnp.zeros((facet_count * CAP, 2, CR, SG), jnp.bfloat16)
        return empty.at[slot_of_subgrid].set(made)
    subgrids = lax.map(band_subgrids, facets)
    slot_flat = block_slot.reshape(-1)
    band_flat = block_band.reshape(-1)
    offset_flat = block_offset.reshape(-1)
    weight_flat = block_weight.reshape(-1)
    pos_flat = vis_pos.reshape(-1, 2, vis_pos.shape[-1])
    zero = jnp.zeros((), jnp.int32)

    def one_block(index):
        facet_of = (index // VB % facet_count).astype(jnp.int32)
        lower_band = band_flat[index].astype(jnp.int32)
        slot = (facet_of * CAP + slot_flat[index]).astype(jnp.int32)
        start = offset_flat[index].astype(jnp.int32)
        lower = lax.dynamic_slice(subgrids, (lower_band, slot, zero, zero, start), (1, 1, 2, CR, PC))[0, 0]
        upper = lax.dynamic_slice(subgrids, (lower_band + 1, slot, zero, zero, start), (1, 1, 2, CR, PC))[0, 0]
        weight = weight_flat[index]
        patch = (1.0 - weight) * lower.astype(jnp.float32) + weight * upper.astype(jnp.float32)
        return degrid_block(patch, pos_flat[index])
    visible = lax.map(one_block, jnp.arange(band_count * facet_count * VB, dtype=jnp.int32))
    return (subgrids, visible.reshape(vis_pos.shape))
```

```python
import math

import jax
import jax.numpy as jnp
import numpy as np
from jax import lax
from jax.experimental import pallas as pl
from jax.experimental.pallas import tpu as pltpu
from jax.sharding import PartitionSpec as P

BF = jnp.bfloat16
F32 = jnp.float32
MESH = pl.DeviceIdType.MESH

SR = 128
SL = 4096
SG = 256
CR = 16
PC = 128
NS = 96
VB = 4
NV = 2048
NX, NY, NC = 4, 8, 2
NF = NX * NY * NC
NB = 8
COLS = SG // NF
CHUNK = NF // NX
K1 = 64
KH = K1 // CR
K2 = 32
SIGMA = 1.5


def tables():
    n = np.arange(SL)
    c = np.arange(SG)
    d = np.exp(2j * np.pi * ((c[None, :] * n[:, None]) % SL) / SL).sum(1)
    d = d / (math.sqrt(SL) * math.sqrt(SG))
    lanes = np.arange(2 * SL)
    first = np.stack([d[(16 * col - lanes) % SL] for col in range(2 * COLS)])
    first = first.reshape(2, COLS, 2 * SL)
    base = np.stack([first.real, first.imag], axis=1).reshape(4 * COLS, 2 * SL)

    k1 = np.arange(K1)
    f = np.arange(NF)
    w = np.exp(-2j * np.pi * ((k1[:, None] * f[None, :]) % NF) / NF) / math.sqrt(NF)
    w = w.reshape(KH, CR, NF)
    eye = np.eye(COLS)
    parts = [[w.real, -w.imag], [w.imag, w.real]]
    over_facets = np.zeros((2, KH, COLS, CR, NF, 2, COLS))
    for o in range(2):
        for i in range(2):
            over_facets[o, :, :, :, :, i, :] = np.einsum("hrf,cd->hcrfd", parts[o][i], eye)
    over_facets = over_facets.reshape(2 * KH * COLS * CR, NF * 2 * COLS)

    j = np.arange(SR)
    t = np.exp(-2j * np.pi * (k1[:, None] * j[None, :]) / (K1 * SR)).reshape(KH, 1, CR, SR)
    t = np.broadcast_to(t, (KH, COLS, CR, SR)).reshape(KH * COLS * CR, SR)
    twiddle = np.stack([t.real, t.imag])

    k2 = np.arange(K2)
    v = np.exp(-2j * np.pi * ((k2[:, None] * j[None, :]) % SR) / SR) / math.sqrt(SR)
    v = np.where(k2[:, None] < NS // KH, v, 0)
    over_rows = np.concatenate([v.real, v.imag], axis=1)

    order = np.zeros((NS, KH * K2))
    for s in range(NS):
        order[s, (s % KH) * K2 + s // KH] = 1.0
    return base, over_facets, twiddle, over_rows, order


def wait_for(ref, sem):
    pltpu.make_async_copy(ref, ref, sem).wait()


def kernel(
    facets, window, base, over_facets, twiddle, over_rows, order, slots,
    block_slot, block_band, block_offset, block_weight, vis_pos,
    subgrids, visible,
    raw, table, base_v, win_v, over_facets_v, twiddle_v, over_rows_v, order_v, slots_v,
    slot_s, band_s, offset_s, weight_s, pos_v,
    send1, recv1, send2, held, pick, col_kernel, row_kernel,
    raw_sem, const_sem, own_sem, send1_sem, recv1_sem, send2_sem, recv2_sem, send3_sem, recv3_sem,
):
    me = lax.axis_index("facet")
    band = lax.axis_index("band")
    x = me // (NY * NC)
    y = (me // NC) % NY
    core = me % NC

    def facet_at(dx, i):
        k = i // 2
        dy = 4 + (k // 2 + k % 2) * (1 - 2 * (k % 2))
        px = lax.rem(x + dx, NX)
        py = lax.rem(y + dy, NY)
        pc = lax.rem(core + 1 - i % 2, NC)
        return (px * NY + py) * NC + pc

    def each_peer(dx, do):
        def body(i, carry):
            do(facet_at(dx, i))
            return carry

        lax.fori_loop(0, CHUNK if dx else CHUNK - 1, body, 0)

    barrier = pltpu.get_barrier_semaphore()
    for dx in (2, 1, 3, 0):
        each_peer(
            dx,
            lambda p: pl.semaphore_signal(
                barrier, inc=1, device_id=(band, p), device_id_type=MESH
            ),
        )
    for i in range(1, NB):
        pl.semaphore_signal(
            barrier, inc=1, device_id=(lax.rem(band + i, NB), me), device_id_type=MESH
        )

    consts = [
        pltpu.make_async_copy(src, dst, const_sem.at[i])
        for i, (src, dst) in enumerate(
            (
                (base, base_v), (window, win_v), (over_facets, over_facets_v),
                (twiddle, twiddle_v), (over_rows, over_rows_v), (order, order_v),
                (slots, slots_v), (block_slot, slot_s), (block_band, band_s),
                (block_offset, offset_s), (block_weight, weight_s), (vis_pos, pos_v),
            )
        )
    ]
    consts[0].start()
    quarter = SL // 4
    loads = [
        pltpu.make_async_copy(
            facets.at[:, :, pl.ds(quarter * i, quarter)],
            raw.at[:, :, pl.ds(quarter * i, quarter)],
            raw_sem.at[i],
        )
        for i in range(4)
    ]
    consts[1].start()
    for copy in loads:
        copy.start()
    for copy in consts[2:]:
        copy.start()

    consts[0].wait()

    def fill(a, carry):
        start = pl.multiple_of(SL - 128 * a, 128)
        row = pl.multiple_of(16 * a, 16)
        table[pl.ds(row, 16), :] = base_v[:, pl.ds(start, SL)]
        return carry

    lax.fori_loop(0, 4 * NF * COLS * 2 // 64, fill, 0)

    consts[1].wait()
    total = None
    for i in range(4):
        loads[i].wait()
        cut = pl.ds(quarter * i, quarter)
        windowed = (raw[:, :, cut].astype(F32) * win_v[:, cut][None]).astype(BF)
        windowed = windowed.reshape(2 * SR, quarter)
        product = lax.dot_general(
            table[:, cut], windowed, (((1,), (1,)), ((), ())), preferred_element_type=F32
        )
        total = product if total is None else total + product
    from_real = total[:, :SR].reshape(NF, 2 * COLS, SR)
    from_imag = total[:, SR:].reshape(NF, 2 * COLS, SR)
    swapped = pltpu.roll(from_imag, COLS, 1)
    part = lax.broadcasted_iota(jnp.int32, swapped.shape, 1)
    send1[...] = (from_real + jnp.where(part < COLS, -swapped, swapped)).astype(BF)

    pl.semaphore_wait(barrier, NF - 1 + NB - 1)

    for dx in (2, 1, 3, 0):
        each_peer(
            dx,
            lambda p: pltpu.make_async_remote_copy(
                send1.at[p], recv1.at[me], send1_sem, recv1_sem,
                device_id=(band, p), device_id_type=MESH,
            ).start(),
        )
    own1 = pltpu.make_async_copy(send1.at[me], recv1.at[me], own_sem.at[0])
    own1.start()

    for copy in consts[2:]:
        copy.wait()
    named = lax.broadcasted_iota(jnp.int32, (2 * NF, NS), 0) == slots_v[...]
    choose = jnp.dot(
        jnp.where(named, 1.0, 0.0).astype(BF), order_v[...], preferred_element_type=F32
    ).astype(BF)
    scale = 1.0 / (2.0 * SIGMA * SIGMA)
    rows = lax.broadcasted_iota(jnp.int32, (CR, NV), 0).astype(F32)
    cols = lax.broadcasted_iota(jnp.int32, (PC, 512), 0).astype(F32)
    for v in range(VB):
        dr = rows - pos_v[v, 0:1, :] * (CR - 1)
        row_kernel[v] = jnp.exp(-dr * dr * scale)

        def gauss(i, carry, v=v):
            cut = pl.ds(pl.multiple_of(512 * i, 512), 512)
            dc = cols - pos_v[v, 1:2, cut] * (PC - 1)
            col_kernel[v // 2, pl.ds(PC * (v % 2), PC), cut] = jnp.exp(-dc * dc * scale).astype(BF)
            return carry

        lax.fori_loop(0, NV // 512, gauss, 0)
        source = lax.broadcasted_iota(jnp.int32, (2 * NF, PC), 0)
        q = lax.broadcasted_iota(jnp.int32, (2 * NF, PC), 1)
        for c in range(COLS):
            hit = ((source // 2) * COLS + c == q + offset_s[0, 0, v]) & (
                source % 2 == slot_s[0, 0, v]
            )
            pick[v, :, pl.ds(PC * c, PC)] = jnp.where(hit, 1.0, 0.0).astype(BF)

    own1.wait()
    wait_for(recv1.at[pl.ds(0, NF - 1)], recv1_sem)
    arrived = recv1[...].astype(F32).reshape(NF * 2 * COLS, SR).astype(BF)
    half = KH * COLS * CR
    over = jnp.dot(over_facets_v[...], arrived, preferred_element_type=F32)
    yr, yi = over[:half], over[half:]
    tr, ti = twiddle_v[0], twiddle_v[1]
    zr = (yr * tr - yi * ti).astype(BF)
    zi = (yi * tr + yr * ti).astype(BF)
    block = COLS * CR
    turned = jnp.concatenate(
        [
            piece
            for h in range(KH)
            for piece in (
                jnp.concatenate([zr[h * block : (h + 1) * block], -zi[h * block : (h + 1) * block]], 1),
                jnp.concatenate([zi[h * block : (h + 1) * block], zr[h * block : (h + 1) * block]], 1),
            )
        ],
        axis=0,
    )
    grid = lax.dot_general(
        over_rows_v[...], turned, (((1,), (1,)), ((), ())), preferred_element_type=F32
    )
    by_subgrid = jnp.concatenate(
        [grid[:, 2 * block * h : 2 * block * (h + 1)] for h in range(KH)], axis=0
    ).astype(BF)
    by_slot = jnp.dot(choose, by_subgrid, preferred_element_type=F32)
    send2[...] = by_slot.reshape(NF, 2, 2 * block).astype(BF)

    for dx in (2, 1, 3, 0):
        each_peer(
            dx,
            lambda p, dx=dx: pltpu.make_async_remote_copy(
                send2.at[p], held.at[band, me], send2_sem, recv2_sem.at[dx],
                device_id=(band, p), device_id_type=MESH,
            ).start(),
        )
    own2 = pltpu.make_async_copy(send2.at[me], held.at[band, me], own_sem.at[1])
    own2.start()
    own2.wait()
    for dx in (0, 1, 3, 2):
        count = CHUNK if dx else CHUNK - 1
        wait_for(send2.at[pl.ds(0, count)], recv2_sem.at[dx])
        piece = pl.ds(pl.multiple_of(lax.rem(x + NX - dx, NX) * CHUNK, CHUNK), CHUNK)
        for i in (4, 3, 5, 2, 6, 1, 7):
            pltpu.make_async_remote_copy(
                held.at[band, piece], held.at[band, piece], send3_sem, recv3_sem,
                device_id=(lax.rem(band + i, NB), me), device_id_type=MESH,
            ).start()

    def spread(values, selector):
        return lax.dot_general(
            values, selector, (((0,), (0,)), ((), ())), preferred_element_type=F32
        )

    def joined(rows_by, width):
        return [
            sum(
                rows_by[p * block + c * CR : p * block + (c + 1) * CR, width * c : width * (c + 1)]
                for c in range(COLS)
            )
            for p in range(2)
        ]

    own = held[band].astype(F32).reshape(2 * NF, 2 * block).astype(BF)
    source = lax.broadcasted_iota(jnp.int32, (2 * NF, SG), 0)
    column = lax.broadcasted_iota(jnp.int32, (2 * NF, SG), 1)
    for slot in range(2):
        selector = jnp.concatenate(
            [
                jnp.where(
                    ((source // 2) * COLS + c == column) & (source % 2 == slot), 1.0, 0.0
                ).astype(BF)
                for c in range(COLS)
            ],
            axis=1,
        )
        pieces = joined(spread(own, selector), SG)
        for p in range(2):
            subgrids[slot, p] = pieces[p].astype(BF)

    wait_for(held.at[pl.ds(0, NB - 1)], recv3_sem)
    nothing = jnp.zeros((2 * CR, PC), BF)
    for pair in range(VB // 2):
        patches = []
        for v in (2 * pair, 2 * pair + 1):
            lo = band_s[0, 0, v]
            weight = weight_s[0, 0, v]
            mixed = (1.0 - weight) * held[lo].astype(F32) + weight * held[lo + 1].astype(F32)
            mixed = mixed.reshape(2 * NF, 2 * block).astype(BF)
            pieces = joined(spread(mixed, pick[v]), PC)
            patches.append(jnp.concatenate(pieces, axis=0).astype(BF))
        left = jnp.concatenate(
            [
                jnp.concatenate([patches[0], nothing], 1),
                jnp.concatenate([nothing, patches[1]], 1),
            ],
            axis=0,
        )
        summed = jnp.dot(left, col_kernel[pair], preferred_element_type=F32)
        for b in range(2):
            v = 2 * pair + b
            for p in range(2):
                at = (2 * b + p) * CR
                visible[v, p : p + 1, :] = jnp.sum(
                    summed[at : at + CR] * row_kernel[v], axis=0, keepdims=True
                )

    wait_for(send1.at[pl.ds(0, NF - 1)], send1_sem)
    wait_for(send2.at[pl.ds(0, NF - 1)], send2_sem)
    wait_for(held.at[pl.ds(0, NB - 1)], send3_sem)


def local(
    facets, col_window, slot_of_subgrid, block_slot, block_band, block_offset, block_weight, vis_pos
):
    base, over_facets, twiddle, over_rows, order = tables()
    anywhere = pl.BlockSpec(memory_space=pl.ANY)
    whole = pl.BlockSpec(memory_space=pltpu.VMEM)
    dma = pltpu.SemaphoreType.DMA
    vmem = pltpu.VMEM
    half = KH * COLS * CR
    args = (
        facets[0, 0],
        col_window[None],
        jnp.asarray(base, BF),
        jnp.asarray(over_facets, BF),
        jnp.asarray(twiddle, F32),
        jnp.asarray(over_rows, BF),
        jnp.asarray(order, BF),
        slot_of_subgrid[None],
        block_slot,
        block_band,
        block_offset,
        block_weight,
        vis_pos[0, 0],
    )
    subgrids, visible = pl.pallas_call(
        kernel,
        out_shape=(
            jax.ShapeDtypeStruct((2, 2, CR, SG), BF),
            jax.ShapeDtypeStruct((VB, 2, NV), F32),
        ),
        in_specs=[anywhere] * len(args),
        out_specs=(whole, whole),
        scratch_shapes=[
            vmem((2, SR, SL), BF),
            vmem((NF * 2 * COLS, SL), BF),
            vmem((4 * COLS, 2 * SL), BF),
            vmem((1, SL), F32),
            vmem((2 * half, NF * 2 * COLS), BF),
            vmem((2, half, SR), F32),
            vmem((K2, 2 * SR), BF),
            vmem((NS, KH * K2), BF),
            vmem((1, NS), jnp.int32),
            pltpu.SMEM((1, 1, VB), jnp.int32),
            pltpu.SMEM((1, 1, VB), jnp.int32),
            pltpu.SMEM((1, 1, VB), jnp.int32),
            pltpu.SMEM((1, 1, VB), F32),
            vmem((VB, 2, NV), F32),
            vmem((NF, 2 * COLS, SR), BF),
            vmem((NF, 2 * COLS, SR), BF),
            vmem((NF, 2, 2 * COLS * CR), BF),
            vmem((NB, NF, 2, 2 * COLS * CR), BF),
            vmem((VB, 2 * NF, COLS * PC), BF),
            vmem((VB // 2, 2 * PC, NV), BF),
            vmem((VB, CR, NV), F32),
            dma((4,)),
            dma((12,)),
            dma((2,)),
            dma,
            dma,
            dma,
            dma((NX,)),
            dma,
            dma,
        ],
        compiler_params=pltpu.CompilerParams(collective_id=0, has_side_effects=True),
        name="column_pass",
    )(*args)
    return subgrids[None], visible[None, None]


def solution(mesh):
    in_specs = (
        P("band", "facet", None, None, None),
        P(),
        P(),
        P("band", "facet", None),
        P("band", "facet", None),
        P("band", "facet", None),
        P("band", "facet", None),
        P("band", "facet", None, None, None),
    )
    out_specs = (P("band", "facet", None, None, None), P("band", "facet", None, None, None))
    return jax.shard_map(local, mesh=mesh, in_specs=in_specs, out_specs=out_specs, check_vma=False)
```

```python
import math

import jax
import jax.numpy as jnp
import numpy as np
from jax import lax
from jax.experimental import pallas as pl
from jax.experimental.pallas import tpu as pltpu
from jax.sharding import PartitionSpec as P

BF = jnp.bfloat16
F32 = jnp.float32
MESH = pl.DeviceIdType.MESH

SR = 128
SL = 4096
SG = 256
CR = 16
PC = 128
NS = 96
VB = 4
NV = 2048
NX, NY, NC = 4, 8, 2
NF = NX * NY * NC
NB = 8
COLS = SG // NF
CHUNK = NF // NX
K1 = 64
KH = K1 // CR
K2 = 32
SIGMA = 1.5
BLOCK = COLS * CR
HALF = KH * BLOCK
PEERS = sorted(
    (
        (dx, dy, dc)
        for dx in range(NX)
        for dy in range(NY)
        for dc in range(NC)
        if dx or dy or dc
    ),
    key=lambda t: -(4 * min(t[0], NX - t[0]) + 4 * min(t[1], NY - t[1]) + t[2]),
)


def tables():
    n = np.arange(SL)
    c = np.arange(SG)
    d = np.exp(2j * np.pi * ((c[None, :] * n[:, None]) % SL) / SL).sum(1)
    d = d / (math.sqrt(SL) * math.sqrt(SG))
    lanes = np.arange(2 * SL)
    first = np.stack([d[(16 * col - lanes) % SL] for col in range(2 * COLS)])
    first = first.reshape(2, COLS, 2 * SL)
    base = np.stack([first.real, first.imag], axis=1).reshape(4 * COLS, 2 * SL)

    k1 = np.arange(K1)
    f = np.arange(NF)
    w = np.exp(-2j * np.pi * ((k1[:, None] * f[None, :]) % NF) / NF) / math.sqrt(NF)
    w = w.reshape(KH, CR, NF)
    eye = np.eye(COLS)
    parts = [[w.real, -w.imag], [w.imag, w.real]]
    over_facets = np.zeros((2, KH, COLS, CR, NF, 2, COLS))
    for o in range(2):
        for i in range(2):
            over_facets[o, :, :, :, :, i, :] = np.einsum("hrf,cd->hcrfd", parts[o][i], eye)
    over_facets = over_facets.reshape(2 * KH * COLS * CR, NF * 2 * COLS)

    j = np.arange(SR)
    t = np.exp(-2j * np.pi * (k1[:, None] * j[None, :]) / (K1 * SR)).reshape(KH, 1, CR, SR)
    t = np.broadcast_to(t, (KH, COLS, CR, SR)).reshape(KH * COLS * CR, SR)
    twiddle = np.stack([t.real, t.imag])

    k2 = np.arange(K2)
    v = np.exp(-2j * np.pi * ((k2[:, None] * j[None, :]) % SR) / SR) / math.sqrt(SR)
    v = np.where(k2[:, None] < NS // KH, v, 0)
    over_rows = np.concatenate([v.real, v.imag], axis=1)

    order = np.zeros((NS, KH * K2))
    for s in range(NS):
        order[s, (s % KH) * K2 + s // KH] = 1.0
    return base, over_facets, twiddle, over_rows, order


def wait_for(ref, sem):
    pltpu.make_async_copy(ref, ref, sem).wait()


def spread(values, selector):
    return lax.dot_general(
        values, selector, (((0,), (0,)), ((), ())), preferred_element_type=F32
    )


def joined(rows_by, width):
    return [
        sum(
            rows_by[p * BLOCK + c * CR : p * BLOCK + (c + 1) * CR, width * c : width * (c + 1)]
            for c in range(COLS)
        )
        for p in range(2)
    ]


def exchange_kernel(
    facets, window, base, over_facets, twiddle, over_rows, order, slots,
    block_slot, block_offset, vis_pos,
    held, pick, col_kernel, row_kernel, subgrids,
    raw, table, base_v, win_v, over_facets_v, twiddle_v, over_rows_v, order_v, slots_v,
    slot_s, offset_s, pos_v,
    send1, recv1, send2,
    raw_sem, const_sem, own_sem, send1_sem, recv1_sem, send2_sem, recv2_sem, send3_sem, recv3_sem,
):
    me = lax.axis_index("facet")
    band = lax.axis_index("band")
    x = me // (NY * NC)
    y = (me // NC) % NY
    core = me % NC

    rows_of = [lax.rem(x + dx, NX) * (NY * NC) for dx in range(NX)]
    places = [lax.rem(y + dy, NY) * NC for dy in range(NY)]
    cores = [core, 1 - core]

    def each_peer(do):
        for dx, dy, dc in PEERS:
            do(dx, rows_of[dx] + places[dy] + cores[dc])

    consts = [
        pltpu.make_async_copy(src, dst, const_sem.at[i])
        for i, (src, dst) in enumerate(
            (
                (base, base_v), (window, win_v), (over_facets, over_facets_v),
                (twiddle, twiddle_v), (over_rows, over_rows_v), (order, order_v),
                (slots, slots_v), (block_slot, slot_s), (block_offset, offset_s),
                (vis_pos, pos_v),
            )
        )
    ]
    consts[0].start()
    quarter = SL // 4
    loads = [
        pltpu.make_async_copy(
            facets.at[:, :, pl.ds(quarter * i, quarter)],
            raw.at[:, :, pl.ds(quarter * i, quarter)],
            raw_sem.at[i],
        )
        for i in range(4)
    ]
    consts[1].start()
    for copy in loads:
        copy.start()

    barrier = pltpu.get_barrier_semaphore()
    each_peer(
        lambda dx, p: pl.semaphore_signal(
            barrier, inc=1, device_id=(band, p), device_id_type=MESH
        )
    )
    for i in range(1, NB):
        pl.semaphore_signal(
            barrier, inc=1, device_id=(lax.rem(band + i, NB), me), device_id_type=MESH
        )
    for copy in consts[2:]:
        copy.start()

    consts[0].wait()
    for a in range(SG // (2 * COLS)):
        table[16 * a : 16 * (a + 1), :] = base_v[:, SL - 128 * a : 2 * SL - 128 * a]

    consts[1].wait()
    total = None
    for i in range(4):
        loads[i].wait()
        cut = pl.ds(quarter * i, quarter)
        windowed = (raw[:, :, cut].astype(F32) * win_v[:, cut][None]).astype(BF)
        windowed = windowed.reshape(2 * SR, quarter)
        product = lax.dot_general(
            table[:, cut], windowed, (((1,), (1,)), ((), ())), preferred_element_type=F32
        )
        total = product if total is None else total + product
    from_real = total[:, :SR].reshape(NF, 2 * COLS, SR)
    from_imag = total[:, SR:].reshape(NF, 2 * COLS, SR)
    swapped = pltpu.roll(from_imag, COLS, 1)
    part = lax.broadcasted_iota(jnp.int32, swapped.shape, 1)
    send1[...] = (from_real + jnp.where(part < COLS, -swapped, swapped)).astype(BF)

    pl.semaphore_wait(barrier, NF - 1 + NB - 1)

    each_peer(
        lambda dx, p: pltpu.make_async_remote_copy(
            send1.at[p], recv1.at[me], send1_sem, recv1_sem,
            device_id=(band, p), device_id_type=MESH,
        ).start()
    )
    own1 = pltpu.make_async_copy(send1.at[me], recv1.at[me], own_sem.at[0])
    own1.start()

    for copy in consts[2:]:
        copy.wait()
    named = lax.broadcasted_iota(jnp.int32, (2 * NF, NS), 0) == slots_v[...]
    choose = jnp.dot(
        jnp.where(named, 1.0, 0.0).astype(BF), order_v[...], preferred_element_type=F32
    ).astype(BF)
    scale = 1.0 / (2.0 * SIGMA * SIGMA)
    rows = lax.broadcasted_iota(jnp.int32, (CR, NV), 0).astype(F32)
    cols = lax.broadcasted_iota(jnp.int32, (PC, 512), 0).astype(F32)
    for v in range(VB):
        dr = rows - pos_v[v, 0:1, :] * (CR - 1)
        row_kernel[v] = jnp.exp(-dr * dr * scale)

        def gauss(i, carry, v=v):
            cut = pl.ds(pl.multiple_of(512 * i, 512), 512)
            dc = cols - pos_v[v, 1:2, cut] * (PC - 1)
            col_kernel[v // 2, pl.ds(PC * (v % 2), PC), cut] = jnp.exp(-dc * dc * scale).astype(BF)
            return carry

        lax.fori_loop(0, NV // 512, gauss, 0)
        source = lax.broadcasted_iota(jnp.int32, (2 * NF, PC), 0)
        q = lax.broadcasted_iota(jnp.int32, (2 * NF, PC), 1)
        for c in range(COLS):
            hit = ((source // 2) * COLS + c == q + offset_s[0, 0, v]) & (
                source % 2 == slot_s[0, 0, v]
            )
            pick[v, :, pl.ds(PC * c, PC)] = jnp.where(hit, 1.0, 0.0).astype(BF)

    own1.wait()
    wait_for(recv1.at[pl.ds(0, NF - 1)], recv1_sem)
    arrived = recv1[...].astype(F32).reshape(NF * 2 * COLS, SR).astype(BF)
    over = jnp.dot(over_facets_v[...], arrived, preferred_element_type=F32)
    yr, yi = over[:HALF], over[HALF:]
    tr, ti = twiddle_v[0], twiddle_v[1]
    zr = (yr * tr - yi * ti).astype(BF)
    zi = (yi * tr + yr * ti).astype(BF)
    turned = jnp.concatenate(
        [
            piece
            for h in range(KH)
            for piece in (
                jnp.concatenate([zr[h * BLOCK : (h + 1) * BLOCK], -zi[h * BLOCK : (h + 1) * BLOCK]], 1),
                jnp.concatenate([zi[h * BLOCK : (h + 1) * BLOCK], zr[h * BLOCK : (h + 1) * BLOCK]], 1),
            )
        ],
        axis=0,
    )
    grid = lax.dot_general(
        over_rows_v[...], turned, (((1,), (1,)), ((), ())), preferred_element_type=F32
    )
    by_subgrid = jnp.concatenate(
        [grid[:, 2 * BLOCK * h : 2 * BLOCK * (h + 1)] for h in range(KH)], axis=0
    ).astype(BF)
    by_slot = jnp.dot(choose, by_subgrid, preferred_element_type=F32)
    send2[...] = by_slot.reshape(NF, 2, 2 * BLOCK).astype(BF)

    each_peer(
        lambda dx, p: pltpu.make_async_remote_copy(
            send2.at[p], held.at[band, me], send2_sem, recv2_sem.at[dx],
            device_id=(band, p), device_id_type=MESH,
        ).start()
    )
    own2 = pltpu.make_async_copy(send2.at[me], held.at[band, me], own_sem.at[1])
    own2.start()
    own2.wait()
    for dx in (0, 1, 3, 2):
        count = CHUNK if dx else CHUNK - 1
        wait_for(send2.at[pl.ds(0, count)], recv2_sem.at[dx])
        piece = pl.ds(pl.multiple_of(lax.rem(x + NX - dx, NX) * CHUNK, CHUNK), CHUNK)
        for to in range(NB):

            @pl.when(band != to)
            def _(to=to, piece=piece):
                pltpu.make_async_remote_copy(
                    held.at[band, piece], held.at[band, piece], send3_sem, recv3_sem,
                    device_id=(to, me), device_id_type=MESH,
                ).start()

    own = held[band].astype(F32).reshape(2 * NF, 2 * BLOCK).astype(BF)
    source = lax.broadcasted_iota(jnp.int32, (2 * NF, SG), 0)
    column = lax.broadcasted_iota(jnp.int32, (2 * NF, SG), 1)
    for slot in range(2):
        selector = jnp.concatenate(
            [
                jnp.where(
                    ((source // 2) * COLS + c == column) & (source % 2 == slot), 1.0, 0.0
                ).astype(BF)
                for c in range(COLS)
            ],
            axis=1,
        )
        pieces = joined(spread(own, selector), SG)
        for p in range(2):
            subgrids[slot, p] = pieces[p].astype(BF)

    wait_for(held.at[pl.ds(0, NB - 1)], recv3_sem)
    wait_for(send1.at[pl.ds(0, NF - 1)], send1_sem)
    wait_for(send2.at[pl.ds(0, NF - 1)], send2_sem)
    wait_for(held.at[pl.ds(0, NB - 1)], send3_sem)


def degrid_kernel(block_band, block_weight, held, pick, col_kernel, row_kernel, own, subgrids, visible):
    subgrids[...] = own[...]
    nothing = jnp.zeros((2 * CR, PC), BF)
    for pair in range(VB // 2):
        patches = []
        for v in (2 * pair, 2 * pair + 1):
            lo = block_band[0, 0, v]
            weight = block_weight[0, 0, v]
            mixed = (1.0 - weight) * held[lo].astype(F32) + weight * held[lo + 1].astype(F32)
            mixed = mixed.reshape(2 * NF, 2 * BLOCK).astype(BF)
            pieces = joined(spread(mixed, pick[v]), PC)
            patches.append(jnp.concatenate(pieces, axis=0).astype(BF))
        left = jnp.concatenate(
            [
                jnp.concatenate([patches[0], nothing], 1),
                jnp.concatenate([nothing, patches[1]], 1),
            ],
            axis=0,
        )
        summed = jnp.dot(left, col_kernel[pair], preferred_element_type=F32)
        for b in range(2):
            v = 2 * pair + b
            for p in range(2):
                at = (2 * b + p) * CR
                visible[v, p : p + 1, :] = jnp.sum(
                    summed[at : at + CR] * row_kernel[v], axis=0, keepdims=True
                )


def local(
    facets, col_window, slot_of_subgrid, block_slot, block_band, block_offset, block_weight, vis_pos
):
    base, over_facets, twiddle, over_rows, order = tables()
    anywhere = pl.BlockSpec(memory_space=pltpu.HBM)
    whole = pl.BlockSpec(memory_space=pltpu.VMEM)
    dma = pltpu.SemaphoreType.DMA
    vmem = pltpu.VMEM
    args = (
        facets[0, 0],
        col_window[None],
        jnp.asarray(base, BF),
        jnp.asarray(over_facets, BF),
        jnp.asarray(twiddle, F32),
        jnp.asarray(over_rows, BF),
        jnp.asarray(order, BF),
        slot_of_subgrid[None],
        block_slot,
        block_offset,
        vis_pos[0, 0],
    )
    made = pl.pallas_call(
        exchange_kernel,
        out_shape=(
            vmem((NB, NF, 2, 2 * BLOCK), BF),
            vmem((VB, 2 * NF, COLS * PC), BF),
            vmem((VB // 2, 2 * PC, NV), BF),
            vmem((VB, CR, NV), F32),
            vmem((2, 2, CR, SG), BF),
        ),
        in_specs=[anywhere] * len(args),
        out_specs=(whole,) * 5,
        scratch_shapes=[
            vmem((2, SR, SL), BF),
            vmem((NF * 2 * COLS, SL), BF),
            vmem((4 * COLS, 2 * SL), BF),
            vmem((1, SL), F32),
            vmem((2 * HALF, NF * 2 * COLS), BF),
            vmem((2, HALF, SR), F32),
            vmem((K2, 2 * SR), BF),
            vmem((NS, KH * K2), BF),
            vmem((1, NS), jnp.int32),
            pltpu.SMEM((1, 1, VB), jnp.int32),
            pltpu.SMEM((1, 1, VB), jnp.int32),
            vmem((VB, 2, NV), F32),
            vmem((NF, 2 * COLS, SR), BF),
            vmem((NF, 2 * COLS, SR), BF),
            vmem((NF, 2, 2 * BLOCK), BF),
            dma((4,)),
            dma((10,)),
            dma((2,)),
            dma,
            dma,
            dma,
            dma((NX,)),
            dma,
            dma,
        ],
        compiler_params=pltpu.CompilerParams(
            collective_id=0, has_side_effects=True, vmem_limit_bytes=24 * 2**20
        ),
        name="column_pass",
    )(*(pltpu.with_memory_space_constraint(a, pltpu.HBM) for a in args))
    scalars = pl.BlockSpec(memory_space=pltpu.SMEM)
    subgrids, visible = pl.pallas_call(
        degrid_kernel,
        out_shape=(
            jax.ShapeDtypeStruct((2, 2, CR, SG), BF),
            jax.ShapeDtypeStruct((VB, 2, NV), F32),
        ),
        in_specs=[scalars, scalars] + [whole] * 5,
        out_specs=(whole, whole),
        compiler_params=pltpu.CompilerParams(vmem_limit_bytes=24 * 2**20),
        name="degrid",
    )(block_band, block_weight, *made)
    return subgrids[None], visible[None, None]


def solution(mesh):
    in_specs = (
        P("band", "facet", None, None, None),
        P(),
        P(),
        P("band", "facet", None),
        P("band", "facet", None),
        P("band", "facet", None),
        P("band", "facet", None),
        P("band", "facet", None, None, None),
    )
    out_specs = (P("band", "facet", None, None, None), P("band", "facet", None, None, None))
    return jax.shard_map(local, mesh=mesh, in_specs=in_specs, out_specs=out_specs, check_vma=False)
```

```python
import math

import jax
import jax.numpy as jnp
import numpy as np
from jax import lax
from jax.experimental import pallas as pl
from jax.experimental.pallas import tpu as pltpu
from jax.sharding import PartitionSpec as P

BF = jnp.bfloat16
F32 = jnp.float32
MESH = pl.DeviceIdType.MESH

SR = 128
SL = 4096
SG = 256
CR = 16
PC = 128
NS = 96
VB = 4
NV = 2048
NX, NY, NC = 4, 8, 2
NF = NX * NY * NC
NB = 8
COLS = SG // NF
CHUNK = NF // NX
K1 = 64
KH = K1 // CR
K2 = 32
SIGMA = 1.5
BLOCK = COLS * CR
HALF = KH * BLOCK
PEERS = sorted(
    (
        (dx, dy, dc)
        for dx in range(NX)
        for dy in range(NY)
        for dc in range(NC)
        if dx or dy or dc
    ),
    key=lambda t: -(4 * min(t[0], NX - t[0]) + 4 * min(t[1], NY - t[1]) + t[2]),
)


def tables():
    bases = []
    lanes = np.arange(SL) - SL // 2
    for parity in range(2):
        c = np.arange(parity, SG, 2)
        n = np.arange(SL)
        d = np.exp(2j * np.pi * ((c[None, :] * n[:, None]) % SL) / SL).sum(1)
        d = d / (math.sqrt(SL) * math.sqrt(SG))
        first = np.stack([d[(16 * col - lanes) % SL] for col in range(2 * COLS)])
        first = first.reshape(2, COLS, SL)
        bases.append(np.stack([first.real, first.imag], axis=1).reshape(4 * COLS, SL))
    base = np.stack(bases)

    k1 = np.arange(K1)
    f = np.arange(NF)
    w = np.exp(-2j * np.pi * ((k1[:, None] * f[None, :]) % NF) / NF) / math.sqrt(NF)
    w = w.reshape(KH, CR, NF)
    eye = np.eye(COLS)
    parts = [[w.real, -w.imag], [w.imag, w.real]]
    over_facets = np.zeros((2, KH, COLS, CR, NF, 2, COLS))
    for o in range(2):
        for i in range(2):
            over_facets[o, :, :, :, :, i, :] = np.einsum("hrf,cd->hcrfd", parts[o][i], eye)
    over_facets = over_facets.reshape(2 * KH * COLS * CR, NF * 2 * COLS)

    j = np.arange(SR)
    t = np.exp(-2j * np.pi * (k1[:, None] * j[None, :]) / (K1 * SR)).reshape(KH, 1, CR, SR)
    t = np.broadcast_to(t, (KH, COLS, CR, SR)).reshape(KH * COLS * CR, SR)
    twiddle = np.stack([t.real, t.imag])

    k2 = np.arange(K2)
    v = np.exp(-2j * np.pi * ((k2[:, None] * j[None, :]) % SR) / SR) / math.sqrt(SR)
    v = np.where(k2[:, None] < NS // KH, v, 0)
    over_rows = np.concatenate([v.real, v.imag], axis=1)

    order = np.zeros((NS, KH * K2))
    for s in range(NS):
        order[s, (s % KH) * K2 + s // KH] = 1.0
    return base, over_facets, twiddle, over_rows, order


def wait_for(ref, sem):
    pltpu.make_async_copy(ref, ref, sem).wait()


def spread(values, selector):
    return lax.dot_general(
        values, selector, (((0,), (0,)), ((), ())), preferred_element_type=F32
    )


def joined(rows_by, width):
    return [
        sum(
            rows_by[p * BLOCK + c * CR : p * BLOCK + (c + 1) * CR, width * c : width * (c + 1)]
            for c in range(COLS)
        )
        for p in range(2)
    ]


def exchange_kernel(
    facets, window, base, over_facets, twiddle, over_rows, order, slots,
    block_slot, block_offset, vis_pos,
    held, pick, col_kernel, row_kernel, subgrids,
    raw, table, base_v, win_v, over_facets_v, twiddle_v, over_rows_v, order_v, slots_v,
    slot_s, offset_s, pos_v,
    send1, recv1, send2,
    raw_sem, const_sem, own_sem, send1_sem, recv1_sem, send2_sem, recv2_sem, ready,
):
    me = lax.axis_index("facet")
    band = lax.axis_index("band")
    x = me // (NY * NC)
    y = (me // NC) % NY
    core = me % NC
    rows_of = [lax.rem(x + dx, NX) * (NY * NC) for dx in range(NX)]
    places = [lax.rem(y + dy, NY) * NC for dy in range(NY)]
    cores = [core, 1 - core]

    def each_peer(do):
        for dx, dy, dc in PEERS:
            do(dx, rows_of[dx] + places[dy] + cores[dc])

    consts = [
        pltpu.make_async_copy(src, dst, const_sem.at[i])
        for i, (src, dst) in enumerate(
            (
                (base, base_v), (window, win_v), (over_facets, over_facets_v),
                (twiddle, twiddle_v), (over_rows, over_rows_v), (order, order_v),
                (slots, slots_v), (block_slot, slot_s), (block_offset, offset_s),
                (vis_pos, pos_v),
            )
        )
    ]
    consts[0].start()
    eighth = SL // 8
    loads = [
        pltpu.make_async_copy(
            facets.at[:, :, pl.ds(eighth * i, eighth)],
            raw.at[:, :, pl.ds(eighth * i, eighth)],
            raw_sem.at[i],
        )
        for i in range(8)
    ]
    consts[1].start()
    for i in (0, 4, 1, 5, 2, 6, 3, 7):
        loads[i].start()

    barrier = pltpu.get_barrier_semaphore()

    def signal(to_band, to):
        pl.semaphore_signal(barrier, inc=1, device_id=(to_band, to), device_id_type=MESH)

    each_peer(lambda dx, p: signal(band, p))
    for i in range(1, NB):
        signal(lax.rem(band + i, NB), me)

    for copy in consts[2:]:
        copy.start()

    consts[0].wait()
    mid = SL // 2
    for a in range(SG // (4 * COLS)):
        for parity in range(2):
            table[parity, 16 * a : 16 * (a + 1), :] = base_v[
                parity, :, mid - 128 * a : 2 * mid - 128 * a
            ]

    consts[1].wait()
    totals = [None, None]
    for i in range(4):
        halves = []
        for j in (i, i + 4):
            loads[j].wait()
            cut = pl.ds(eighth * j, eighth)
            halves.append(raw[:, :, cut].astype(F32) * win_v[:, cut][None])
        for parity in range(2):
            mixed = halves[0] - halves[1] if parity else halves[0] + halves[1]
            mixed = mixed.astype(BF).reshape(2 * SR, eighth)
            product = lax.dot_general(
                table[parity, :, eighth * i : eighth * (i + 1)], mixed,
                (((1,), (1,)), ((), ())), preferred_element_type=F32,
            )
            totals[parity] = product if i == 0 else totals[parity] + product
    part = lax.broadcasted_iota(jnp.int32, (NF // 2, 2 * COLS, SR), 1)
    for upper in range(2):
        total = totals[0] - totals[1] if upper else totals[0] + totals[1]
        from_real = total[:, :SR].reshape(NF // 2, 2 * COLS, SR)
        from_imag = total[:, SR:].reshape(NF // 2, 2 * COLS, SR)
        swapped = pltpu.roll(from_imag, COLS, 1)
        send1[upper * (NF // 2) : (upper + 1) * (NF // 2)] = (
            from_real + jnp.where(part < COLS, -swapped, swapped)
        ).astype(BF)

    pl.semaphore_wait(barrier, NF - 1 + NB - 1)

    each_peer(
        lambda dx, p: pltpu.make_async_remote_copy(
            send1.at[p], recv1.at[me], send1_sem, recv1_sem,
            device_id=(band, p), device_id_type=MESH,
        ).start()
    )
    own1 = pltpu.make_async_copy(send1.at[me], recv1.at[me], own_sem.at[0])
    own1.start()
    for i in range(1, NB):
        pl.semaphore_signal(
            ready, inc=1, device_id=(lax.rem(band + i, NB), me), device_id_type=MESH
        )

    for copy in consts[2:]:
        copy.wait()
    named = lax.broadcasted_iota(jnp.int32, (2 * NF, NS), 0) == slots_v[...]
    choose = jnp.dot(
        jnp.where(named, 1.0, 0.0).astype(BF), order_v[...], preferred_element_type=F32
    ).astype(BF)
    scale = 1.0 / (2.0 * SIGMA * SIGMA)
    rows = lax.broadcasted_iota(jnp.int32, (CR, NV), 0).astype(F32)
    cols = lax.broadcasted_iota(jnp.int32, (PC, 512), 0).astype(F32)
    for v in range(VB):
        dr = rows - pos_v[v, 0:1, :] * (CR - 1)
        row_kernel[v] = jnp.exp(-dr * dr * scale)

        def gauss(i, carry, v=v):
            cut = pl.ds(pl.multiple_of(512 * i, 512), 512)
            dc = cols - pos_v[v, 1:2, cut] * (PC - 1)
            col_kernel[v // 2, pl.ds(PC * (v % 2), PC), cut] = jnp.exp(-dc * dc * scale).astype(BF)
            return carry

        lax.fori_loop(0, NV // 512, gauss, 0)
        source = lax.broadcasted_iota(jnp.int32, (2 * NF, PC), 0)
        q = lax.broadcasted_iota(jnp.int32, (2 * NF, PC), 1)
        for c in range(COLS):
            hit = ((source // 2) * COLS + c == q + offset_s[0, 0, v]) & (
                source % 2 == slot_s[0, 0, v]
            )
            pick[v, :, pl.ds(PC * c, PC)] = jnp.where(hit, 1.0, 0.0).astype(BF)

    own1.wait()
    wait_for(recv1.at[pl.ds(0, NF - 1)], recv1_sem)
    arrived = recv1[...].astype(F32).reshape(NF * 2 * COLS, SR).astype(BF)
    over = jnp.dot(over_facets_v[...], arrived, preferred_element_type=F32)
    yr, yi = over[:HALF], over[HALF:]
    tr, ti = twiddle_v[0], twiddle_v[1]
    zr = (yr * tr - yi * ti).astype(BF)
    zi = (yi * tr + yr * ti).astype(BF)
    turned = []
    for h in range(KH):
        cut = slice(h * BLOCK, (h + 1) * BLOCK)
        turned.append(jnp.concatenate([zr[cut], -zi[cut]], 1))
        turned.append(jnp.concatenate([zi[cut], zr[cut]], 1))
    grid = lax.dot_general(
        over_rows_v[...], jnp.concatenate(turned, 0),
        (((1,), (1,)), ((), ())), preferred_element_type=F32,
    )
    by_subgrid = jnp.concatenate(
        [grid[:, 2 * BLOCK * h : 2 * BLOCK * (h + 1)] for h in range(KH)], axis=0
    ).astype(BF)
    by_slot = jnp.dot(choose, by_subgrid, preferred_element_type=F32)
    send2[...] = by_slot.reshape(NF, 2, 2 * BLOCK).astype(BF)

    pl.semaphore_wait(ready, NB - 1)

    def send_slots(to_band, carry):
        away = (to_band != band).astype(jnp.int32)

        def send(to):
            pltpu.make_async_remote_copy(
                send2.at[to], held.at[band, me], send2_sem.at[away], recv2_sem.at[away],
                device_id=(to_band, to), device_id_type=MESH,
            ).start()

        each_peer(lambda dx, p: send(p))

        @pl.when(to_band != band)
        def _():
            send(me)

        return carry

    lax.fori_loop(0, NB, send_slots, 0)
    own2 = pltpu.make_async_copy(send2.at[me], held.at[band, me], own_sem.at[1])
    own2.start()
    own2.wait()
    wait_for(send2.at[pl.ds(0, NF - 1)], recv2_sem.at[0])

    own = held[band].astype(F32).reshape(2 * NF, 2 * BLOCK).astype(BF)
    source = lax.broadcasted_iota(jnp.int32, (2 * NF, SG), 0)
    column = lax.broadcasted_iota(jnp.int32, (2 * NF, SG), 1)
    for slot in range(2):
        selector = jnp.concatenate(
            [
                jnp.where(
                    ((source // 2) * COLS + c == column) & (source % 2 == slot), 1.0, 0.0
                ).astype(BF)
                for c in range(COLS)
            ],
            axis=1,
        )
        pieces = joined(spread(own, selector), SG)
        for p in range(2):
            subgrids[slot, p] = pieces[p].astype(BF)

    wait_for(held.at[pl.ds(0, NB - 1)], recv2_sem.at[1])
    wait_for(send1.at[pl.ds(0, NF - 1)], send1_sem)
    wait_for(send2.at[pl.ds(0, NF - 1)], send2_sem.at[0])
    wait_for(held.at[pl.ds(0, NB - 1)], send2_sem.at[1])


def degrid_kernel(block_band, block_weight, held, pick, col_kernel, row_kernel, own, subgrids, visible):
    subgrids[...] = own[...]
    nothing = jnp.zeros((2 * CR, PC), BF)
    for pair in range(VB // 2):
        patches = []
        for v in (2 * pair, 2 * pair + 1):
            lo = block_band[0, 0, v]
            weight = block_weight[0, 0, v]
            mixed = (1.0 - weight) * held[lo].astype(F32) + weight * held[lo + 1].astype(F32)
            mixed = mixed.reshape(2 * NF, 2 * BLOCK).astype(BF)
            pieces = joined(spread(mixed, pick[v]), PC)
            patches.append(jnp.concatenate(pieces, axis=0).astype(BF))
        left = jnp.concatenate(
            [
                jnp.concatenate([patches[0], nothing], 1),
                jnp.concatenate([nothing, patches[1]], 1),
            ],
            axis=0,
        )
        summed = jnp.dot(left, col_kernel[pair], preferred_element_type=F32)
        for b in range(2):
            v = 2 * pair + b
            for p in range(2):
                at = (2 * b + p) * CR
                visible[v, p : p + 1, :] = jnp.sum(
                    summed[at : at + CR] * row_kernel[v], axis=0, keepdims=True
                )


def local(
    facets, col_window, slot_of_subgrid, block_slot, block_band, block_offset, block_weight, vis_pos
):
    base, over_facets, twiddle, over_rows, order = tables()
    anywhere = pl.BlockSpec(memory_space=pltpu.HBM)
    whole = pl.BlockSpec(memory_space=pltpu.VMEM)
    dma = pltpu.SemaphoreType.DMA
    vmem = pltpu.VMEM
    args = (
        facets[0, 0],
        col_window[None],
        jnp.asarray(base, BF),
        jnp.asarray(over_facets, BF),
        jnp.asarray(twiddle, F32),
        jnp.asarray(over_rows, BF),
        jnp.asarray(order, BF),
        slot_of_subgrid[None],
        block_slot,
        block_offset,
        vis_pos[0, 0],
    )
    made = pl.pallas_call(
        exchange_kernel,
        out_shape=(
            vmem((NB, NF, 2, 2 * BLOCK), BF),
            vmem((VB, 2 * NF, COLS * PC), BF),
            vmem((VB // 2, 2 * PC, NV), BF),
            vmem((VB, CR, NV), F32),
            vmem((2, 2, CR, SG), BF),
        ),
        in_specs=[anywhere] * len(args),
        out_specs=(whole,) * 5,
        scratch_shapes=[
            vmem((2, SR, SL), BF),
            vmem((2, NF * COLS, SL // 2), BF),
            vmem((2, 4 * COLS, SL), BF),
            vmem((1, SL), F32),
            vmem((2 * HALF, NF * 2 * COLS), BF),
            vmem((2, HALF, SR), F32),
            vmem((K2, 2 * SR), BF),
            vmem((NS, KH * K2), BF),
            vmem((1, NS), jnp.int32),
            pltpu.SMEM((1, 1, VB), jnp.int32),
            pltpu.SMEM((1, 1, VB), jnp.int32),
            vmem((VB, 2, NV), F32),
            vmem((NF, 2 * COLS, SR), BF),
            vmem((NF, 2 * COLS, SR), BF),
            vmem((NF, 2, 2 * BLOCK), BF),
            dma((8,)),
            dma((10,)),
            dma((2,)),
            dma,
            dma,
            dma((2,)),
            dma((2,)),
            pltpu.SemaphoreType.REGULAR,
        ],
        compiler_params=pltpu.CompilerParams(
            collective_id=0, has_side_effects=True, vmem_limit_bytes=24 * 2**20
        ),
        name="column_pass",
    )(*(pltpu.with_memory_space_constraint(a, pltpu.HBM) for a in args))
    scalars = pl.BlockSpec(memory_space=pltpu.SMEM)
    subgrids, visible = pl.pallas_call(
        degrid_kernel,
        out_shape=(
            jax.ShapeDtypeStruct((2, 2, CR, SG), BF),
            jax.ShapeDtypeStruct((VB, 2, NV), F32),
        ),
        in_specs=[scalars, scalars] + [whole] * 5,
        out_specs=(whole, whole),
        compiler_params=pltpu.CompilerParams(vmem_limit_bytes=24 * 2**20),
        name="degrid",
    )(block_band, block_weight, *made)
    return subgrids[None], visible[None, None]


def solution(mesh):
    in_specs = (
        P("band", "facet", None, None, None),
        P(),
        P(),
        P("band", "facet", None),
        P("band", "facet", None),
        P("band", "facet", None),
        P("band", "facet", None),
        P("band", "facet", None, None, None),
    )
    out_specs = (P("band", "facet", None, None, None), P("band", "facet", None, None, None))
    return jax.shard_map(local, mesh=mesh, in_specs=in_specs, out_specs=out_specs, check_vma=False)
```

```python
import math

import jax
import jax.numpy as jnp
import numpy as np
from jax import lax
from jax.experimental import pallas as pl
from jax.experimental.pallas import tpu as pltpu
from jax.sharding import PartitionSpec as P

BF = jnp.bfloat16
F32 = jnp.float32
MESH = pl.DeviceIdType.MESH

SR = 128
SL = 4096
SG = 256
CR = 16
PC = 128
NS = 96
VB = 4
NV = 2048
NX, NY, NC = 4, 8, 2
NF = NX * NY * NC
NB = 8
COLS = SG // NF
CHUNK = NF // NX
K1 = 64
KH = K1 // CR
K2 = 32
SIGMA = 1.5
BLOCK = COLS * CR
HALF = KH * BLOCK
PEERS = sorted(
    (
        (dx, dy, dc)
        for dx in range(NX)
        for dy in range(NY)
        for dc in range(NC)
        if dx or dy or dc
    ),
    key=lambda t: -(4 * min(t[0], NX - t[0]) + 4 * min(t[1], NY - t[1]) + t[2]),
)


def tables():
    bases = []
    lanes = np.arange(SL) - SL // 2
    for parity in range(2):
        c = np.arange(parity, SG, 2)
        n = np.arange(SL)
        d = np.exp(2j * np.pi * ((c[None, :] * n[:, None]) % SL) / SL).sum(1)
        d = d / (math.sqrt(SL) * math.sqrt(SG))
        first = np.stack([d[(16 * col - lanes) % SL] for col in range(2 * COLS)])
        first = first.reshape(2, COLS, SL)
        bases.append(np.stack([first.real, first.imag], axis=1).reshape(4 * COLS, SL))
    base = np.stack(bases)

    k1 = np.arange(K1)
    f = np.arange(NF)
    w = np.exp(-2j * np.pi * ((k1[:, None] * f[None, :]) % NF) / NF) / math.sqrt(NF)
    w = w.reshape(KH, CR, NF)
    eye = np.eye(COLS)
    parts = [[w.real, -w.imag], [w.imag, w.real]]
    over_facets = np.zeros((2, KH, COLS, CR, NF, 2, COLS))
    for o in range(2):
        for i in range(2):
            over_facets[o, :, :, :, :, i, :] = np.einsum("hrf,cd->hcrfd", parts[o][i], eye)
    over_facets = over_facets.reshape(2 * KH * COLS * CR, NF * 2 * COLS)

    j = np.arange(SR)
    t = np.exp(-2j * np.pi * (k1[:, None] * j[None, :]) / (K1 * SR)).reshape(KH, 1, CR, SR)
    t = np.broadcast_to(t, (KH, COLS, CR, SR)).reshape(KH * COLS * CR, SR)
    twiddle = np.stack([t.real, t.imag])

    k2 = np.arange(K2)
    v = np.exp(-2j * np.pi * ((k2[:, None] * j[None, :]) % SR) / SR) / math.sqrt(SR)
    v = np.where(k2[:, None] < NS // KH, v, 0)
    over_rows = np.concatenate([v.real, v.imag], axis=1)

    order = np.zeros((NS, KH * K2))
    for s in range(NS):
        order[s, (s % KH) * K2 + s // KH] = 1.0
    return base, over_facets, twiddle, over_rows, order


def wait_for(ref, sem):
    pltpu.make_async_copy(ref, ref, sem).wait()


def spread(values, selector):
    return lax.dot_general(
        values, selector, (((0,), (0,)), ((), ())), preferred_element_type=F32
    )


def joined(rows_by, width):
    return [
        sum(
            rows_by[p * BLOCK + c * CR : p * BLOCK + (c + 1) * CR, width * c : width * (c + 1)]
            for c in range(COLS)
        )
        for p in range(2)
    ]


def exchange_kernel(
    facets, window, base, over_facets, twiddle, over_rows, order, slots,
    block_slot, block_band, block_offset, block_weight, vis_pos,
    left, col_kernel, row_kernel, subgrids,
    raw, table, base_v, win_v, over_facets_v, twiddle_v, over_rows_v, order_v, slots_v,
    slot_s, band_s, offset_s, weight_s, pos_v,
    send1, recv1, send2, held, pick,
    raw_sem, const_sem, own_sem, send1_sem, recv1_sem, send2_sem, recv2_sem, ready,
):
    me = lax.axis_index("facet")
    band = lax.axis_index("band")
    x = me // (NY * NC)
    y = (me // NC) % NY
    core = me % NC
    rows_of = [lax.rem(x + dx, NX) * (NY * NC) for dx in range(NX)]
    places = [lax.rem(y + dy, NY) * NC for dy in range(NY)]
    cores = [core, 1 - core]

    def each_peer(do):
        for dx, dy, dc in PEERS:
            do(dx, rows_of[dx] + places[dy] + cores[dc])

    consts = [
        pltpu.make_async_copy(src, dst, const_sem.at[i])
        for i, (src, dst) in enumerate(
            (
                (base, base_v), (window, win_v), (over_facets, over_facets_v),
                (twiddle, twiddle_v), (over_rows, over_rows_v), (order, order_v),
                (slots, slots_v), (block_slot, slot_s), (block_band, band_s),
                (block_offset, offset_s), (block_weight, weight_s), (vis_pos, pos_v),
            )
        )
    ]
    consts[0].start()
    eighth = SL // 8
    loads = [
        pltpu.make_async_copy(
            facets.at[:, :, pl.ds(eighth * i, eighth)],
            raw.at[:, :, pl.ds(eighth * i, eighth)],
            raw_sem.at[i],
        )
        for i in range(8)
    ]
    consts[1].start()
    for i in (0, 4, 1, 5, 2, 6, 3, 7):
        loads[i].start()

    barrier = pltpu.get_barrier_semaphore()

    def signal(to_band, to):
        pl.semaphore_signal(barrier, inc=1, device_id=(to_band, to), device_id_type=MESH)

    each_peer(lambda dx, p: signal(band, p))
    for i in range(1, NB):
        signal(lax.rem(band + i, NB), me)

    for copy in consts[2:]:
        copy.start()

    consts[0].wait()
    mid = SL // 2
    for a in range(SG // (4 * COLS)):
        for parity in range(2):
            table[parity, 16 * a : 16 * (a + 1), :] = base_v[
                parity, :, mid - 128 * a : 2 * mid - 128 * a
            ]

    consts[1].wait()
    totals = [None, None]
    for i in range(4):
        halves = []
        for j in (i, i + 4):
            loads[j].wait()
            cut = pl.ds(eighth * j, eighth)
            halves.append(raw[:, :, cut].astype(F32) * win_v[:, cut][None])
        for parity in range(2):
            mixed = halves[0] - halves[1] if parity else halves[0] + halves[1]
            mixed = mixed.astype(BF).reshape(2 * SR, eighth)
            product = lax.dot_general(
                table[parity, :, eighth * i : eighth * (i + 1)], mixed,
                (((1,), (1,)), ((), ())), preferred_element_type=F32,
            )
            totals[parity] = product if i == 0 else totals[parity] + product
    part = lax.broadcasted_iota(jnp.int32, (NF // 2, 2 * COLS, SR), 1)
    for upper in range(2):
        total = totals[0] - totals[1] if upper else totals[0] + totals[1]
        from_real = total[:, :SR].reshape(NF // 2, 2 * COLS, SR)
        from_imag = total[:, SR:].reshape(NF // 2, 2 * COLS, SR)
        swapped = pltpu.roll(from_imag, COLS, 1)
        send1[upper * (NF // 2) : (upper + 1) * (NF // 2)] = (
            from_real + jnp.where(part < COLS, -swapped, swapped)
        ).astype(BF)

    pl.semaphore_wait(barrier, NF - 1 + NB - 1)

    each_peer(
        lambda dx, p: pltpu.make_async_remote_copy(
            send1.at[p], recv1.at[me], send1_sem, recv1_sem,
            device_id=(band, p), device_id_type=MESH,
        ).start()
    )
    own1 = pltpu.make_async_copy(send1.at[me], recv1.at[me], own_sem.at[0])
    own1.start()
    for i in range(1, NB):
        pl.semaphore_signal(
            ready, inc=1, device_id=(lax.rem(band + i, NB), me), device_id_type=MESH
        )

    for copy in consts[2:]:
        copy.wait()
    named = lax.broadcasted_iota(jnp.int32, (2 * NF, NS), 0) == slots_v[...]
    choose = jnp.dot(
        jnp.where(named, 1.0, 0.0).astype(BF), order_v[...], preferred_element_type=F32
    ).astype(BF)
    scale = 1.0 / (2.0 * SIGMA * SIGMA)
    rows = lax.broadcasted_iota(jnp.int32, (CR, NV), 0).astype(F32)
    cols = lax.broadcasted_iota(jnp.int32, (PC, 512), 0).astype(F32)
    for v in range(VB):
        dr = rows - pos_v[v, 0:1, :] * (CR - 1)
        row_kernel[v] = jnp.exp(-dr * dr * scale)

        def gauss(i, carry, v=v):
            cut = pl.ds(pl.multiple_of(512 * i, 512), 512)
            dc = cols - pos_v[v, 1:2, cut] * (PC - 1)
            col_kernel[v // 2, pl.ds(PC * (v % 2), PC), cut] = jnp.exp(-dc * dc * scale).astype(BF)
            return carry

        lax.fori_loop(0, NV // 512, gauss, 0)
        source = lax.broadcasted_iota(jnp.int32, (2 * NF, PC), 0)
        q = lax.broadcasted_iota(jnp.int32, (2 * NF, PC), 1)
        for c in range(COLS):
            hit = ((source // 2) * COLS + c == q + offset_s[0, 0, v]) & (
                source % 2 == slot_s[0, 0, v]
            )
            pick[v, :, pl.ds(PC * c, PC)] = jnp.where(hit, 1.0, 0.0).astype(BF)

    own1.wait()
    wait_for(recv1.at[pl.ds(0, NF - 1)], recv1_sem)
    arrived = recv1[...].astype(F32).reshape(NF * 2 * COLS, SR).astype(BF)
    over = jnp.dot(over_facets_v[...], arrived, preferred_element_type=F32)
    yr, yi = over[:HALF], over[HALF:]
    tr, ti = twiddle_v[0], twiddle_v[1]
    zr = (yr * tr - yi * ti).astype(BF)
    zi = (yi * tr + yr * ti).astype(BF)
    turned = []
    for h in range(KH):
        cut = slice(h * BLOCK, (h + 1) * BLOCK)
        turned.append(jnp.concatenate([zr[cut], -zi[cut]], 1))
        turned.append(jnp.concatenate([zi[cut], zr[cut]], 1))
    grid = lax.dot_general(
        over_rows_v[...], jnp.concatenate(turned, 0),
        (((1,), (1,)), ((), ())), preferred_element_type=F32,
    )
    by_subgrid = jnp.concatenate(
        [grid[:, 2 * BLOCK * h : 2 * BLOCK * (h + 1)] for h in range(KH)], axis=0
    ).astype(BF)
    by_slot = jnp.dot(choose, by_subgrid, preferred_element_type=F32)
    send2[...] = by_slot.reshape(NF, 2, 2 * BLOCK).astype(BF)

    pl.semaphore_wait(ready, NB - 1)

    def send_slots(to_band, carry):
        away = (to_band != band).astype(jnp.int32)

        def send(to):
            pltpu.make_async_remote_copy(
                send2.at[to], held.at[band, me], send2_sem.at[away], recv2_sem.at[away],
                device_id=(to_band, to), device_id_type=MESH,
            ).start()

        each_peer(lambda dx, p: send(p))

        @pl.when(to_band != band)
        def _():
            send(me)

        return carry

    lax.fori_loop(0, NB, send_slots, 0)
    own2 = pltpu.make_async_copy(send2.at[me], held.at[band, me], own_sem.at[1])
    own2.start()
    own2.wait()
    wait_for(send2.at[pl.ds(0, NF - 1)], recv2_sem.at[0])

    own = held[band].astype(F32).reshape(2 * NF, 2 * BLOCK).astype(BF)
    source = lax.broadcasted_iota(jnp.int32, (2 * NF, SG), 0)
    column = lax.broadcasted_iota(jnp.int32, (2 * NF, SG), 1)
    for slot in range(2):
        selector = jnp.concatenate(
            [
                jnp.where(
                    ((source // 2) * COLS + c == column) & (source % 2 == slot), 1.0, 0.0
                ).astype(BF)
                for c in range(COLS)
            ],
            axis=1,
        )
        pieces = joined(spread(own, selector), SG)
        for p in range(2):
            subgrids[slot, p] = pieces[p].astype(BF)

    wait_for(held.at[pl.ds(0, NB - 1)], recv2_sem.at[1])
    nothing = jnp.zeros((2 * CR, PC), BF)
    for pair in range(VB // 2):
        patches = []
        for v in (2 * pair, 2 * pair + 1):
            lo = band_s[0, 0, v]
            weight = weight_s[0, 0, v]
            mixed = (1.0 - weight) * held[lo].astype(F32) + weight * held[lo + 1].astype(F32)
            mixed = mixed.reshape(2 * NF, 2 * BLOCK).astype(BF)
            pieces = joined(spread(mixed, pick[v]), PC)
            patches.append(jnp.concatenate(pieces, axis=0).astype(BF))
        left[pair] = jnp.concatenate(
            [
                jnp.concatenate([patches[0], nothing], 1),
                jnp.concatenate([nothing, patches[1]], 1),
            ],
            axis=0,
        )
    wait_for(send1.at[pl.ds(0, NF - 1)], send1_sem)
    wait_for(send2.at[pl.ds(0, NF - 1)], send2_sem.at[0])
    wait_for(held.at[pl.ds(0, NB - 1)], send2_sem.at[1])


def degrid_kernel(left, col_kernel, row_kernel, own, subgrids, visible, made, sems):
    outs = [pltpu.make_async_copy(own, subgrids, sems.at[0])]
    outs[0].start()
    for pair in range(VB // 2):
        summed = jnp.dot(left[pair], col_kernel[pair], preferred_element_type=F32)
        for b in range(2):
            v = 2 * pair + b
            for p in range(2):
                at = (2 * b + p) * CR
                made[v, p : p + 1, :] = jnp.sum(
                    summed[at : at + CR] * row_kernel[v], axis=0, keepdims=True
                )
        part = pl.ds(2 * pair, 2)
        outs.append(pltpu.make_async_copy(made.at[part], visible.at[part], sems.at[1 + pair]))
        outs[-1].start()
    for copy in outs:
        copy.wait()


def local(
    facets, col_window, slot_of_subgrid, block_slot, block_band, block_offset, block_weight, vis_pos
):
    base, over_facets, twiddle, over_rows, order = tables()
    anywhere = pl.BlockSpec(memory_space=pltpu.HBM)
    whole = pl.BlockSpec(memory_space=pltpu.VMEM)
    dma = pltpu.SemaphoreType.DMA
    vmem = pltpu.VMEM
    args = (
        facets[0, 0],
        col_window[None],
        jnp.asarray(base, BF),
        jnp.asarray(over_facets, BF),
        jnp.asarray(twiddle, F32),
        jnp.asarray(over_rows, BF),
        jnp.asarray(order, BF),
        slot_of_subgrid[None],
        block_slot,
        block_band,
        block_offset,
        block_weight,
        vis_pos[0, 0],
    )
    made = pl.pallas_call(
        exchange_kernel,
        out_shape=(
            vmem((VB // 2, 4 * CR, 2 * PC), BF),
            vmem((VB // 2, 2 * PC, NV), BF),
            vmem((VB, CR, NV), F32),
            vmem((2, 2, CR, SG), BF),
        ),
        in_specs=[anywhere] * len(args),
        out_specs=(whole,) * 4,
        scratch_shapes=[
            vmem((2, SR, SL), BF),
            vmem((2, NF * COLS, SL // 2), BF),
            vmem((2, 4 * COLS, SL), BF),
            vmem((1, SL), F32),
            vmem((2 * HALF, NF * 2 * COLS), BF),
            vmem((2, HALF, SR), F32),
            vmem((K2, 2 * SR), BF),
            vmem((NS, KH * K2), BF),
            vmem((1, NS), jnp.int32),
            pltpu.SMEM((1, 1, VB), jnp.int32),
            pltpu.SMEM((1, 1, VB), jnp.int32),
            pltpu.SMEM((1, 1, VB), jnp.int32),
            pltpu.SMEM((1, 1, VB), F32),
            vmem((VB, 2, NV), F32),
            vmem((NF, 2 * COLS, SR), BF),
            vmem((NF, 2 * COLS, SR), BF),
            vmem((NF, 2, 2 * BLOCK), BF),
            vmem((NB, NF, 2, 2 * BLOCK), BF),
            vmem((VB, 2 * NF, COLS * PC), BF),
            dma((8,)),
            dma((12,)),
            dma((2,)),
            dma,
            dma,
            dma((2,)),
            dma((2,)),
            pltpu.SemaphoreType.REGULAR,
        ],
        compiler_params=pltpu.CompilerParams(
            collective_id=0, has_side_effects=True, vmem_limit_bytes=24 * 2**20
        ),
        name="column_pass",
    )(*(pltpu.with_memory_space_constraint(a, pltpu.HBM) for a in args))
    subgrids, visible = pl.pallas_call(
        degrid_kernel,
        out_shape=(
            jax.ShapeDtypeStruct((2, 2, CR, SG), BF),
            jax.ShapeDtypeStruct((VB, 2, NV), F32),
        ),
        in_specs=[whole] * 4,
        out_specs=(anywhere, anywhere),
        scratch_shapes=[vmem((VB, 2, NV), F32), dma((3,))],
        compiler_params=pltpu.CompilerParams(vmem_limit_bytes=24 * 2**20),
        name="degrid",
    )(*made)
    return subgrids[None], visible[None, None]


def solution(mesh):
    in_specs = (
        P("band", "facet", None, None, None),
        P(),
        P(),
        P("band", "facet", None),
        P("band", "facet", None),
        P("band", "facet", None),
        P("band", "facet", None),
        P("band", "facet", None, None, None),
    )
    out_specs = (P("band", "facet", None, None, None), P("band", "facet", None, None, None))
    return jax.shard_map(local, mesh=mesh, in_specs=in_specs, out_specs=out_specs, check_vma=False)
```

```python
import math

import jax
import jax.numpy as jnp
import numpy as np
from jax import lax
from jax.experimental import pallas as pl
from jax.experimental.pallas import tpu as pltpu
from jax.sharding import PartitionSpec as P

BF = jnp.bfloat16
F32 = jnp.float32
MESH = pl.DeviceIdType.MESH

SR = 128
SL = 4096
SG = 256
CR = 16
PC = 128
NS = 96
VB = 4
NV = 2048
NX, NY, NC = 4, 8, 2
NF = NX * NY * NC
NB = 8
COLS = SG // NF
CHUNK = NF // NX
K1 = 64
KH = K1 // CR
K2 = 32
SIGMA = 1.5
BLOCK = COLS * CR
HALF = KH * BLOCK
PEERS = sorted(
    (
        (dx, dy, dc)
        for dx in range(NX)
        for dy in range(NY)
        for dc in range(NC)
        if dx or dy or dc
    ),
    key=lambda t: -(4 * min(t[0], NX - t[0]) + 4 * min(t[1], NY - t[1]) + t[2]),
)
FIRST = sorted(
    range(NF), key=lambda f: 2 * min(f // NC % NY, NY - f // NC % NY) + f // (NY * NC)
)


def tables():
    bases = []
    lanes = np.arange(SL) - SL // 2
    for parity in range(2):
        c = np.arange(parity, SG, 2)
        n = np.arange(SL)
        d = np.exp(2j * np.pi * ((c[None, :] * n[:, None]) % SL) / SL).sum(1)
        d = d / (math.sqrt(SL) * math.sqrt(SG))
        first = np.stack([d[(16 * col - lanes) % SL] for col in range(2 * COLS)])
        first = first.reshape(2, COLS, SL)
        bases.append(np.stack([first.real, first.imag], axis=1).reshape(4 * COLS, SL))
    base = np.stack(bases)

    k1 = np.arange(K1)
    f = np.arange(NF)
    w = np.exp(-2j * np.pi * ((k1[:, None] * f[None, :]) % NF) / NF) / math.sqrt(NF)
    w = w.reshape(KH, CR, NF)
    eye = np.eye(COLS)
    parts = [[w.real, -w.imag], [w.imag, w.real]]
    over_facets = np.zeros((2, KH, COLS, CR, NF, 2, COLS))
    for o in range(2):
        for i in range(2):
            over_facets[o, :, :, :, :, i, :] = np.einsum("hrf,cd->hcrfd", parts[o][i], eye)
    over_facets = over_facets.reshape(2 * KH * COLS * CR, NF * 2 * COLS)

    j = np.arange(SR)
    t = np.exp(-2j * np.pi * (k1[:, None] * j[None, :]) / (K1 * SR)).reshape(KH, 1, CR, SR)
    t = np.broadcast_to(t, (KH, COLS, CR, SR)).reshape(KH * COLS * CR, SR)
    twiddle = np.stack([t.real, t.imag])

    k2 = np.arange(K2)
    v = np.exp(-2j * np.pi * ((k2[:, None] * j[None, :]) % SR) / SR) / math.sqrt(SR)
    v = np.where(k2[:, None] < NS // KH, v, 0)
    over_rows = np.concatenate([v.real, v.imag], axis=1)

    order = np.zeros((NS, KH * K2))
    for s in range(NS):
        order[s, (s % KH) * K2 + s // KH] = 1.0
    packed = np.zeros((2 * HALF + K2 + NS, NF * 2 * COLS))
    packed[: 2 * HALF] = over_facets
    packed[2 * HALF : 2 * HALF + K2, : 2 * SR] = over_rows
    packed[2 * HALF + K2 :, : KH * K2] = order
    return base, packed, twiddle


def wait_for(ref, sem):
    pltpu.make_async_copy(ref, ref, sem).wait()


def spread(values, selector):
    return lax.dot_general(
        values, selector, (((0,), (0,)), ((), ())), preferred_element_type=F32
    )


def joined(rows_by, width):
    return [
        sum(
            rows_by[p * BLOCK + c * CR : p * BLOCK + (c + 1) * CR, width * c : width * (c + 1)]
            for c in range(COLS)
        )
        for p in range(2)
    ]


def exchange_kernel(
    facets, window, base, packed, twiddle, slots,
    block_slot, block_band, block_offset, block_weight, vis_pos,
    left, col_kernel, row_kernel, subgrids,
    raw, table, base_v, win_v, packed_v, twiddle_v, slots_v,
    slot_s, band_s, offset_s, weight_s, pos_v,
    send1, recv1, send2, held, pick,
    raw_sem, const_sem, own_sem, send1_sem, recv1_sem, send2_sem, recv2_sem, ready,
):
    me = lax.axis_index("facet")
    band = lax.axis_index("band")
    x = me // (NY * NC)
    y = (me // NC) % NY
    core = me % NC
    rows_of = [lax.rem(x + dx, NX) * (NY * NC) for dx in range(NX)]
    places = [lax.rem(y + dy, NY) * NC for dy in range(NY)]
    cores = [core, 1 - core]

    def each_peer(do):
        for dx, dy, dc in PEERS:
            do(dx, rows_of[dx] + places[dy] + cores[dc])

    early_consts = [
        pltpu.make_async_copy(base, base_v, send1_sem),
        pltpu.make_async_copy(window, win_v, own_sem),
    ]
    consts = [
        pltpu.make_async_copy(packed, packed_v, send2_sem.at[0]),
        pltpu.make_async_copy(twiddle, twiddle_v, send2_sem.at[1]),
        pltpu.make_async_copy(slots, slots_v, const_sem.at[0]),
        pltpu.make_async_copy(vis_pos, pos_v, const_sem.at[1]),
    ]
    scalars = [
        pltpu.make_async_copy(block_slot, slot_s, raw_sem.at[0]),
        pltpu.make_async_copy(block_offset, offset_s, raw_sem.at[1]),
        pltpu.make_async_copy(block_band, band_s, raw_sem.at[0]),
        pltpu.make_async_copy(block_weight, weight_s, raw_sem.at[1]),
    ]
    early_consts[0].start()
    early_consts[1].start()
    quarter, eighth = SL // 4, SL // 8
    for i in range(2):
        for j in (i, i + 2):
            cut = pl.ds(quarter * j, quarter)
            pltpu.make_async_copy(facets.at[:, :, cut], raw.at[:, :, cut], raw_sem.at[i]).start()

    barrier = pltpu.get_barrier_semaphore()

    def signal(to_band, to):
        pl.semaphore_signal(barrier, inc=1, device_id=(to_band, to), device_id_type=MESH)

    each_peer(lambda dx, p: signal(band, p))
    for i in range(1, NB):
        signal(lax.rem(band + i, NB), me)

    for copy in consts:
        copy.start()

    early_consts[0].wait()
    mid = SL // 2
    for a in range(SG // (4 * COLS)):
        for parity in range(2):
            table[parity, 16 * a : 16 * (a + 1), :] = base_v[
                parity, :, mid - 128 * a : 2 * mid - 128 * a
            ]

    early_consts[1].wait()
    totals = [None, None]
    for i in range(4):
        halves = []
        if i % 2 == 0:
            wait_for(raw.at[:, :, pl.ds(0, 2 * quarter)], raw_sem.at[i // 2])
        for j in (i, i + 4):
            cut = pl.ds(eighth * j, eighth)
            halves.append(raw[:, :, cut].astype(F32) * win_v[:, cut][None])
        for parity in range(2):
            mixed = halves[0] - halves[1] if parity else halves[0] + halves[1]
            mixed = mixed.astype(BF).reshape(2 * SR, eighth)
            product = lax.dot_general(
                table[parity, :, eighth * i : eighth * (i + 1)], mixed,
                (((1,), (1,)), ((), ())), preferred_element_type=F32,
            )
            totals[parity] = product if i == 0 else totals[parity] + product
    part = lax.broadcasted_iota(jnp.int32, (NF // 2, 2 * COLS, SR), 1)
    for upper in range(2):
        total = totals[0] - totals[1] if upper else totals[0] + totals[1]
        from_real = total[:, :SR].reshape(NF // 2, 2 * COLS, SR)
        from_imag = total[:, SR:].reshape(NF // 2, 2 * COLS, SR)
        swapped = pltpu.roll(from_imag, COLS, 1)
        send1[upper * (NF // 2) : (upper + 1) * (NF // 2)] = (
            from_real + jnp.where(part < COLS, -swapped, swapped)
        ).astype(BF)

    scalars[0].start()
    scalars[1].start()
    pl.semaphore_wait(barrier, NF - 1 + NB - 1)

    each_peer(
        lambda dx, p: pltpu.make_async_remote_copy(
            send1.at[p], recv1.at[me], send1_sem, recv1_sem.at[dx],
            device_id=(band, p), device_id_type=MESH,
        ).start()
    )
    own1 = pltpu.make_async_copy(send1.at[me], recv1.at[me], own_sem)
    own1.start()
    for i in range(1, NB):
        pl.semaphore_signal(
            ready, inc=1, device_id=(lax.rem(band + i, NB), me), device_id_type=MESH
        )

    for copy in consts + scalars[:2]:
        copy.wait()
    scalars[2].start()
    scalars[3].start()
    named = lax.broadcasted_iota(jnp.int32, (2 * NF, NS), 0) == slots_v[...]
    choose = jnp.dot(
        jnp.where(named, 1.0, 0.0).astype(BF), packed_v[2 * HALF + K2 :, : KH * K2], preferred_element_type=F32
    ).astype(BF)
    scale = 1.0 / (2.0 * SIGMA * SIGMA)
    rows = lax.broadcasted_iota(jnp.int32, (CR, NV), 0).astype(F32)
    cols = lax.broadcasted_iota(jnp.int32, (PC, 512), 0).astype(F32)
    for v in range(VB):
        dr = rows - pos_v[v, 0:1, :] * (CR - 1)
        row_kernel[v] = jnp.exp(-dr * dr * scale)

        def gauss(i, carry, v=v):
            cut = pl.ds(pl.multiple_of(512 * i, 512), 512)
            dc = cols - pos_v[v, 1:2, cut] * (PC - 1)
            col_kernel[v // 2, pl.ds(PC * (v % 2), PC), cut] = jnp.exp(-dc * dc * scale).astype(BF)
            return carry

        lax.fori_loop(0, NV // 512, gauss, 0)
        source = lax.broadcasted_iota(jnp.int32, (2 * NF, PC), 0)
        q = lax.broadcasted_iota(jnp.int32, (2 * NF, PC), 1)
        for c in range(COLS):
            hit = ((source // 2) * COLS + c == q + offset_s[0, 0, v]) & (
                source % 2 == slot_s[0, 0, v]
            )
            pick[v, :, pl.ds(PC * c, PC)] = jnp.where(hit, 1.0, 0.0).astype(BF)

    scalars[2].wait()
    scalars[3].wait()

    own1.wait()
    over = None
    for dx in (0, 1, 3, 2):
        count = CHUNK if dx else CHUNK - 1
        row = pl.multiple_of(lax.rem(x + NX - dx, NX) * CHUNK, CHUNK)
        wait_for(recv1.at[pl.ds(0, count)], recv1_sem.at[dx])
        arrived = recv1[pl.ds(row, CHUNK)].astype(F32).reshape(CHUNK * 2 * COLS, SR).astype(BF)
        lanes = pl.ds(pl.multiple_of(row * 2 * COLS, CHUNK * 2 * COLS), CHUNK * 2 * COLS)
        product = jnp.dot(
            packed_v[: 2 * HALF, lanes], arrived, preferred_element_type=F32
        )
        over = product if over is None else over + product
    yr, yi = over[:HALF], over[HALF:]
    tr, ti = twiddle_v[0], twiddle_v[1]
    zr = (yr * tr - yi * ti).astype(BF)
    zi = (yi * tr + yr * ti).astype(BF)
    turned = []
    for h in range(KH):
        cut = slice(h * BLOCK, (h + 1) * BLOCK)
        turned.append(jnp.concatenate([zr[cut], -zi[cut]], 1))
        turned.append(jnp.concatenate([zi[cut], zr[cut]], 1))
    grid = lax.dot_general(
        packed_v[2 * HALF : 2 * HALF + K2, : 2 * SR], jnp.concatenate(turned, 0),
        (((1,), (1,)), ((), ())), preferred_element_type=F32,
    )
    by_subgrid = jnp.concatenate(
        [grid[:, 2 * BLOCK * h : 2 * BLOCK * (h + 1)] for h in range(KH)], axis=0
    ).astype(BF)
    by_slot = jnp.dot(choose, by_subgrid, preferred_element_type=F32)
    send2[...] = by_slot.reshape(NF, 2, 2 * BLOCK).astype(BF)

    pl.semaphore_wait(ready, NB - 1)

    def send_slots(to_band, carry):
        away = (to_band != band).astype(jnp.int32)

        def send(to):
            pltpu.make_async_remote_copy(
                send2.at[to], held.at[band, me], send2_sem.at[away], recv2_sem.at[away],
                device_id=(to_band, to), device_id_type=MESH,
            ).start()

        @pl.when(to_band == band)
        def _():
            each_peer(lambda dx, p: send(p))

        @pl.when(to_band != band)
        def _():
            for to in FIRST:
                send(to)

        return carry

    lax.fori_loop(0, NB, send_slots, 0)
    own2 = pltpu.make_async_copy(send2.at[me], held.at[band, me], own_sem)
    own2.start()
    own2.wait()
    wait_for(send2.at[pl.ds(0, NF - 1)], recv2_sem.at[0])

    own = held[band].astype(F32).reshape(2 * NF, 2 * BLOCK).astype(BF)
    source = lax.broadcasted_iota(jnp.int32, (2 * NF, SG), 0)
    column = lax.broadcasted_iota(jnp.int32, (2 * NF, SG), 1)
    for slot in range(2):
        selector = jnp.concatenate(
            [
                jnp.where(
                    ((source // 2) * COLS + c == column) & (source % 2 == slot), 1.0, 0.0
                ).astype(BF)
                for c in range(COLS)
            ],
            axis=1,
        )
        pieces = joined(spread(own, selector), SG)
        for p in range(2):
            subgrids[slot, p] = pieces[p].astype(BF)

    wait_for(held.at[pl.ds(0, NB - 1)], recv2_sem.at[1])
    nothing = jnp.zeros((2 * CR, PC), BF)
    for pair in range(VB // 2):
        patches = []
        for v in (2 * pair, 2 * pair + 1):
            lo = band_s[0, 0, v]
            weight = weight_s[0, 0, v]
            mixed = (1.0 - weight) * held[lo].astype(F32) + weight * held[lo + 1].astype(F32)
            mixed = mixed.reshape(2 * NF, 2 * BLOCK).astype(BF)
            pieces = joined(spread(mixed, pick[v]), PC)
            patches.append(jnp.concatenate(pieces, axis=0).astype(BF))
        left[pair] = jnp.concatenate(
            [
                jnp.concatenate([patches[0], nothing], 1),
                jnp.concatenate([nothing, patches[1]], 1),
            ],
            axis=0,
        )
    wait_for(send1.at[pl.ds(0, NF - 1)], send1_sem)
    wait_for(send2.at[pl.ds(0, NF - 1)], send2_sem.at[0])
    wait_for(held.at[pl.ds(0, NB - 1)], send2_sem.at[1])


def degrid_kernel(left, col_kernel, row_kernel, own, subgrids, visible, made, sems):
    outs = [pltpu.make_async_copy(own, subgrids, sems.at[0])]
    outs[0].start()
    for pair in range(VB // 2):
        summed = jnp.dot(left[pair], col_kernel[pair], preferred_element_type=F32)
        for b in range(2):
            v = 2 * pair + b
            for p in range(2):
                at = (2 * b + p) * CR
                made[v, p : p + 1, :] = jnp.sum(
                    summed[at : at + CR] * row_kernel[v], axis=0, keepdims=True
                )
        part = pl.ds(2 * pair, 2)
        outs.append(pltpu.make_async_copy(made.at[part], visible.at[part], sems.at[1 + pair]))
        outs[-1].start()
    for copy in outs:
        copy.wait()


def local(
    facets, col_window, slot_of_subgrid, block_slot, block_band, block_offset, block_weight, vis_pos
):
    base, packed, twiddle = tables()
    anywhere = pl.BlockSpec(memory_space=pltpu.HBM)
    whole = pl.BlockSpec(memory_space=pltpu.VMEM)
    dma = pltpu.SemaphoreType.DMA
    vmem = pltpu.VMEM
    args = (
        facets[0, 0],
        col_window[None],
        jnp.asarray(base, BF),
        jnp.asarray(packed, BF),
        jnp.asarray(twiddle, F32),
        slot_of_subgrid[None],
        block_slot,
        block_band,
        block_offset,
        block_weight,
        vis_pos[0, 0],
    )
    made = pl.pallas_call(
        exchange_kernel,
        out_shape=(
            vmem((VB // 2, 4 * CR, 2 * PC), BF),
            vmem((VB // 2, 2 * PC, NV), BF),
            vmem((VB, CR, NV), F32),
            vmem((2, 2, CR, SG), BF),
        ),
        in_specs=[anywhere] * len(args),
        out_specs=(whole,) * 4,
        scratch_shapes=[
            vmem((2, SR, SL), BF),
            vmem((2, NF * COLS, SL // 2), BF),
            vmem((2, 4 * COLS, SL), BF),
            vmem((1, SL), F32),
            vmem((2 * HALF + K2 + NS, NF * 2 * COLS), BF),
            vmem((2, HALF, SR), F32),
            vmem((1, NS), jnp.int32),
            pltpu.SMEM((1, 1, VB), jnp.int32),
            pltpu.SMEM((1, 1, VB), jnp.int32),
            pltpu.SMEM((1, 1, VB), jnp.int32),
            pltpu.SMEM((1, 1, VB), F32),
            vmem((VB, 2, NV), F32),
            vmem((NF, 2 * COLS, SR), BF),
            vmem((NF, 2 * COLS, SR), BF),
            vmem((NF, 2, 2 * BLOCK), BF),
            vmem((NB, NF, 2, 2 * BLOCK), BF),
            vmem((VB, 2 * NF, COLS * PC), BF),
            dma((2,)),
            dma((2,)),
            dma,
            dma,
            dma((NX,)),
            dma((2,)),
            dma((2,)),
            pltpu.SemaphoreType.REGULAR,
        ],
        compiler_params=pltpu.CompilerParams(
            collective_id=0, has_side_effects=True, vmem_limit_bytes=24 * 2**20
        ),
        name="column_pass",
    )(*(pltpu.with_memory_space_constraint(a, pltpu.HBM) for a in args))
    subgrids, visible = pl.pallas_call(
        degrid_kernel,
        out_shape=(
            jax.ShapeDtypeStruct((2, 2, CR, SG), BF),
            jax.ShapeDtypeStruct((VB, 2, NV), F32),
        ),
        in_specs=[whole] * 4,
        out_specs=(anywhere, anywhere),
        scratch_shapes=[vmem((VB, 2, NV), F32), dma((3,))],
        compiler_params=pltpu.CompilerParams(vmem_limit_bytes=24 * 2**20),
        name="degrid",
    )(*made)
    return subgrids[None], visible[None, None]


def solution(mesh):
    in_specs = (
        P("band", "facet", None, None, None),
        P(),
        P(),
        P("band", "facet", None),
        P("band", "facet", None),
        P("band", "facet", None),
        P("band", "facet", None),
        P("band", "facet", None, None, None),
    )
    out_specs = (P("band", "facet", None, None, None), P("band", "facet", None, None, None))
    return jax.shard_map(local, mesh=mesh, in_specs=in_specs, out_specs=out_specs, check_vma=False)
```
